256 devices in a mesh: row: 16 (over z, core), col: 8 (over x_hi, y), lrn: 2 (over x_lo).
Axes of the slice: x: 4 (x_hi: 2, x_lo: 2; x = x_hi * 2 + x_lo), y: 4, z: 8, core: 2. Of those that a mesh axis runs over, the one named last changes fastest.
Arguments:
- responses: int32 [4096, 16384], P('lrn', ('row', 'col')), may hold values 0 or 1
- observed: int32 [4096, 16384], P('lrn', ('row', 'col')), may hold values from 0 to 1, as said below
- qmatrix: int32 [16384, 8], P(('row', 'col')), may hold values from 0 to 1
- guess: float32 [16384], P(('row', 'col')), may hold values from 0.05 to 0.35
- slip: float32 [16384], P(('row', 'col')), may hold values from 0.05 to 0.35
Outputs:
- q3_scaled: float32 [16384, 16384], P('row', ('col', 'lrn'))
The draws below stay inside these ranges and needn't reach their ends.
Inputs may be any that keep to these rules, and one draw needn't show every extreme that they name: Some items have no observed response from any learner.
All inputs are finite; a program needn't handle non-finite values. No bound on the sum of `responses` on one device may be relied on, other than what follows from the above.
Results may differ from the reference program's by a relative error of at most 0.008.
Values may be sent and summed in bfloat16 or wider, within the bound.
No kernel may reach another device: no remote copies, remote signals or barrier semaphores. Data moves between devices by JAX's collectives and lax.ppermute only.
A program may use at most 128 MiB of HBM per device.

```python
import math
import jax
import jax.numpy as jnp
from jax import lax

J = 16384
ATTRS = 8
PROFILES = 256
LEARNERS = 4096


def draw_observed(key, part):
    learner = jnp.arange(LEARNERS, dtype=jnp.int32)
    threshold = 100 + 800 * learner // max(LEARNERS - 1, 1)
    rolls = jax.random.randint(jax.random.fold_in(key, 11), (LEARNERS, J), 0, 1000)
    base = rolls < threshold[:, None]
    silent = jax.random.randint(jax.random.fold_in(key, 12), (J,), 0, 64) == 0
    forced = jax.random.randint(jax.random.fold_in(key, 13), (), 0, J)
    silent = silent | (jnp.arange(J, dtype=jnp.int32) == forced)
    return jnp.where(silent[None, :], 0, base.astype(jnp.int32)).astype(jnp.int32)


def place_ends(result, stream_key, smallest, top_value):
    extent = result.shape
    place = [jax.random.randint(jax.random.fold_in(stream_key, axis), (), 0, extent[axis]) for axis in range(len(extent))]
    result = result.at[tuple(place)].set(smallest)
    longest = extent.index(max(extent))
    place[longest] = (place[longest] + 1) % extent[longest]
    return result.at[tuple(place)].set(top_value)


def steps_of(stream_key, extent, split, smallest, high):
    level, own = 1.0, jax.random.fold_in(stream_key, 6)
    for position, blocks in split:
        heights = jnp.exp(jax.random.uniform(jax.random.fold_in(own, position), (blocks,), jnp.float32, smallest / len(split), high / len(split)))
        level = level * jnp.repeat(heights, extent[position] // blocks).reshape([-1 if axis == position else 1 for axis in range(len(extent))])
    return level


def setup_inputs(seed: int = 0) -> dict:
    keys = jax.random.split(jax.random.key(seed), 6)
    responses = place_ends((jax.random.randint(keys[0], (LEARNERS, J), 0, 2) < 1).astype(jnp.int32), jax.random.fold_in(keys[0], 1), 0, 1)
    observed = draw_observed(jax.random.fold_in(keys[5], 71), 0)
    qmatrix = place_ends(jax.random.randint(keys[2], (J, ATTRS), 0, 2), jax.random.fold_in(keys[2], 1), 0, 1).astype(jnp.int32)
    guess = jnp.clip(jnp.exp(math.log(0.35) - 1.9459101 * jax.random.uniform(keys[3], (J,), jnp.float32) ** steps_of(keys[3], (J,), ((0, 128),), -0.2, 0.2)), 0.05, 0.35)
    slip = jnp.clip(jnp.exp(math.log(0.35) - 1.9459101 * jax.random.uniform(keys[4], (J,), jnp.float32) ** steps_of(keys[4], (J,), ((0, 128),), -0.2, 0.2)), 0.05, 0.35)
    return {"responses": responses, "observed": observed, "qmatrix": qmatrix, "guess": guess, "slip": slip}


def success(qmatrix, guess, slip):
    codes = jnp.arange(PROFILES, dtype=jnp.int32)
    powers = jnp.arange(ATTRS, dtype=jnp.int32)
    bits = (codes[None, :] >> powers[:, None] & 1).astype(jnp.float32)
    lacking = jnp.dot(qmatrix.astype(jnp.float32), 1.0 - bits, precision=lax.Precision.HIGHEST)
    return jnp.where(lacking == 0.0, 1.0 - slip[:, None], guess[:, None])

def reference(responses, observed, qmatrix, guess, slip):
    prob = success(qmatrix, guess, slip)
    answered = responses.astype(jnp.float32)
    seen = observed.astype(jnp.float32)
    loglik = jnp.dot(seen * answered, jnp.log(prob), precision=lax.Precision.HIGHEST)
    loglik = loglik + jnp.dot(seen * (1.0 - answered), jnp.log(1.0 - prob), precision=lax.Precision.HIGHEST)
    posterior = jax.nn.softmax(loglik, axis=1).astype(jnp.bfloat16)
    expected = jnp.dot(posterior, prob.astype(jnp.bfloat16).T, preferred_element_type=jnp.float32)
    resid = seen * (answered - expected)
    count = jnp.maximum(lax.optimization_barrier(jnp.sum(seen, axis=0)), 1.0)
    mean = lax.optimization_barrier(jnp.sum(resid, axis=0)) / count
    var = lax.optimization_barrier(jnp.sum(resid * resid, axis=0)) / count - mean * mean
    zres = (seen * (resid - mean) * lax.rsqrt(var + 1e-06) * lax.rsqrt(count)).astype(jnp.bfloat16)
    wide = zres.astype(jnp.float32)
    gram = jnp.dot(wide.T, wide, precision=lax.Precision.HIGHEST)
    return gram * jnp.sqrt(jnp.float32(LEARNERS))
```

```python
import jax
import jax.numpy as jnp
from jax import lax
from jax.sharding import Mesh, PartitionSpec as P

ATTRS = 8
PROFILES = 256

ROW = ("z", "k")
COL = ("xh", "y")
PLANE = ("xh", "y", "xl")
X = ("xh", "xl")


def shift(x, axis, n, by):
    return lax.ppermute(x, axis, [(i, (i + by) % n) for i in range(n)])


def triple(x):
    high = lax.reduce_precision(x, 8, 7)
    rest = x - high
    middle = lax.reduce_precision(rest, 8, 7)
    return high, middle, rest - middle


def ring(x, axis):
    half = x.shape[0] // 2
    before = shift(x, axis, 4, 1)
    after = shift(x, axis, 4, -1)
    low = shift(before[:half], axis, 4, 1)
    high = shift(after[half:], axis, 4, -1)
    return before, after, low, high


def place(panel, block, start):
    return lax.dynamic_update_slice(panel, block, [jnp.int32(s) for s in start])


def spread_plane(z):
    chunks, rows, items = z.shape
    half = chunks // 2
    x, y = lax.axis_index(X), lax.axis_index("y")
    panel = jnp.zeros((chunks, 4, 4, rows, items), z.dtype)

    line = jnp.zeros((half, 4, rows, items), z.dtype)
    mine = z[:half]
    before, after, low, high = ring(mine, X)
    line = place(line, mine[:, None], (0, x, 0, 0))
    line = place(line, before[:, None], (0, (x + 3) % 4, 0, 0))
    line = place(line, after[:, None], (0, (x + 1) % 4, 0, 0))
    line = place(line, low[:, None], (0, (x + 2) % 4, 0, 0))
    line = place(line, high[:, None], (half // 2, (x + 2) % 4, 0, 0))
    tall = jnp.zeros((half, 4, rows, items), z.dtype)
    mine = z[half:]
    before, after, low, high = ring(mine, "y")
    tall = place(tall, mine[:, None], (0, y, 0, 0))
    tall = place(tall, before[:, None], (0, (y + 3) % 4, 0, 0))
    tall = place(tall, after[:, None], (0, (y + 1) % 4, 0, 0))
    tall = place(tall, low[:, None], (0, (y + 2) % 4, 0, 0))
    tall = place(tall, high[:, None], (half // 2, (y + 2) % 4, 0, 0))

    before, after, low, high = ring(line, "y")
    panel = place(panel, line[:, None], (0, y, 0, 0, 0))
    panel = place(panel, before[:, None], (0, (y + 3) % 4, 0, 0, 0))
    panel = place(panel, after[:, None], (0, (y + 1) % 4, 0, 0, 0))
    panel = place(panel, low[:, None], (0, (y + 2) % 4, 0, 0, 0))
    panel = place(panel, high[:, None], (half // 2, (y + 2) % 4, 0, 0, 0))
    before, after, low, high = ring(tall, X)
    panel = place(panel, tall[:, :, None], (half, 0, x, 0, 0))
    panel = place(panel, before[:, :, None], (half, 0, (x + 3) % 4, 0, 0))
    panel = place(panel, after[:, :, None], (half, 0, (x + 1) % 4, 0, 0))
    panel = place(panel, low[:, :, None], (half, 0, (x + 2) % 4, 0, 0))
    panel = place(panel, high[:, :, None], (half + half // 2, 0, (x + 2) % 4, 0, 0))
    return panel


def swap(x, axis):
    return lax.all_to_all(x, axis, 0, 0, tiled=True)


def shards(responses, observed, qmatrix, guess, slip):
    learners, items = responses.shape
    cols, rows = 8, 16
    part = learners // cols
    chunk = part // rows

    right = (responses * observed).astype(jnp.bfloat16).reshape(cols, part, items)
    seen = observed.astype(jnp.bfloat16).reshape(cols, part, items)
    table = jnp.concatenate(
        [qmatrix.astype(jnp.float32).T, jnp.stack(triple(guess) + triple(slip)), jnp.zeros((2, items))]
    ).astype(jnp.bfloat16)
    table = jnp.broadcast_to(table, (cols,) + table.shape)
    mixed = swap(jnp.concatenate([right, seen, table], axis=1), COL)
    mixed = mixed.transpose(1, 0, 2).reshape(2 * part + 16, cols * items)
    right, seen, table = mixed[:part], mixed[part : 2 * part], mixed[2 * part :].astype(jnp.float32)
    needs = table[:ATTRS]
    guess = table[8] + table[9] + table[10]
    slip = table[11] + table[12] + table[13]

    codes = jnp.arange(PROFILES, dtype=jnp.int32)
    powers = jnp.arange(ATTRS, dtype=jnp.int32)
    bits = (codes[:, None] >> powers[None, :] & 1).astype(jnp.float32)
    lacking = jnp.dot(1.0 - bits, needs, precision=lax.Precision.HIGHEST)
    prob = jnp.where(lacking == 0.0, 1.0 - slip, guess)
    log0 = jnp.log(1.0 - prob)
    weights = jnp.concatenate([jnp.log(prob) - log0, log0], axis=1)
    data = jnp.concatenate([right, seen], axis=1)
    loglik = sum(
        lax.dot_general(data, w.astype(jnp.bfloat16), (((1,), (1,)), ((), ())), preferred_element_type=jnp.float32)
        for w in triple(weights)
    )
    loglik = jnp.sum(swap(loglik, ROW).reshape(rows, chunk, PROFILES), axis=0)
    posterior = jax.nn.softmax(loglik, axis=1).astype(jnp.bfloat16)
    posterior = swap(jnp.broadcast_to(posterior, (rows, chunk, PROFILES)), ROW).reshape(part, PROFILES)

    expected = jnp.dot(posterior, prob.astype(jnp.bfloat16), preferred_element_type=jnp.float32)
    seen = seen.astype(jnp.float32)
    resid = right.astype(jnp.float32) - seen * expected
    sums = jnp.stack([jnp.sum(seen, axis=0), jnp.sum(resid, axis=0), jnp.sum(resid * resid, axis=0)])
    sums = jnp.sum(swap(jnp.broadcast_to(sums, (16,) + sums.shape), PLANE), axis=0)
    count = jnp.maximum(sums[0], 1.0)
    mean = sums[1] / count
    var = sums[2] / count - mean * mean
    root = jnp.sqrt(jnp.sqrt(jnp.float32(learners * 2)))
    zres = (seen * (resid - mean) * (lax.rsqrt(var + 1e-06) * lax.rsqrt(count) * root)).astype(jnp.bfloat16)

    zres = zres.reshape(rows, chunk, cols * items)
    turned = swap(swap(zres, ROW), PLANE)
    turned = turned.reshape(2, 4, 2, chunk, cols * items).transpose(1, 0, 2, 3, 4)
    columns = lax.all_gather(turned, ROW)
    panel = spread_plane(zres)
    flat = (rows * 16 * chunk, cols * items)
    return lax.dot_general(
        panel.reshape(flat), columns.reshape(flat), (((0,), (0,)), ((), ())), preferred_element_type=jnp.float32
    )


def solution(mesh):
    named = Mesh(mesh.devices.reshape(8, 2, 2, 4, 2), ("z", "k", "xh", "y", "xl"))
    items = ROW + COL
    placed = (P("xl", items), P("xl", items), P(items, None), P(items), P(items))
    return jax.shard_map(shards, mesh=named, in_specs=placed, out_specs=P(ROW, PLANE), check_vma=False)
```

```python
import jax
import jax.numpy as jnp
from jax import lax
from jax.experimental import pallas as pl
from jax.experimental.pallas import tpu as pltpu
from jax.sharding import Mesh, PartitionSpec as P

ATTRS = 8
PROFILES = 256

ROW = ("z", "k")
COL = ("xh", "y")
PLANE = ("xh", "y", "xl")
X = ("xh", "xl")


def shift(x, axis, n, by):
    return lax.ppermute(x, axis, [(i, (i + by) % n) for i in range(n)])


def triple(x):
    high = lax.reduce_precision(x, 8, 7)
    rest = x - high
    middle = lax.reduce_precision(rest, 8, 7)
    return high, middle, rest - middle


def around(x, axis):
    return shift(x, axis, 4, 1), shift(x, axis, 4, -1), shift(x, axis, 4, 2)


def other_core(x):
    return lax.ppermute(x, "k", [(0, 1), (1, 0)])


def neighbours(x, axis):
    return shift(x, axis, 4, 1), shift(x, axis, 4, -1)


def across(before, after, axis):
    half = before.shape[0] // 2
    return shift(before[:half], axis, 4, 1), shift(after[half:], axis, 4, -1)


def gram_kernel(upper, lower, columns, out, left):
    step = pl.program_id(0)
    for at in range(4):
        three, far = ((upper[:3], upper[3 + at]) if at < 2 else (lower[:3], lower[3 + at - 2]))

        @pl.when(step == at)
        def _():
            for i, piece in enumerate(tuple(three) + (far,)):
                if at < 2:
                    left[:, i] = piece[...]
                else:
                    left[:, :, i] = piece[...]

    term = lax.dot_general(
        left[...].reshape(columns.shape), columns[...], (((0,), (0,)), ((), ())), preferred_element_type=jnp.float32
    )

    @pl.when(step == 0)
    def _():
        out[...] = term

    @pl.when(step > 0)
    def _():
        out[...] += term


def gram(upper, lower, columns):
    learners, items = columns.shape
    rows = upper[0].shape[2]
    steps = 4
    block = (learners // steps // (16 * rows), 4, rows, items)
    pair = [
        pl.BlockSpec(block, lambda j: (jnp.minimum(j, 1), 0, 0, 0)),
        pl.BlockSpec(block, lambda j: (jnp.maximum(j - 2, 0), 0, 0, 0)),
    ]
    far = pl.BlockSpec(block, lambda j: (0, 0, 0, 0))
    return pl.pallas_call(
        lambda *refs: gram_kernel(refs[:5], refs[5:10], *refs[10:]),
        grid=(steps,),
        in_specs=[pair[0]] * 3 + [far] * 2 + [pair[1]] * 3 + [far] * 2
        + [pl.BlockSpec((learners // steps, items), lambda j: (j, 0))],
        out_specs=pl.BlockSpec((items, items), lambda j: (0, 0)),
        out_shape=jax.ShapeDtypeStruct((items, items), jnp.float32),
        scratch_shapes=[pltpu.VMEM((block[0], 4, 4, rows, items), jnp.bfloat16)],
        compiler_params=pltpu.CompilerParams(
            dimension_semantics=("arbitrary",), vmem_limit_bytes=56 * 2**20
        ),
        name="gram",
    )(*upper, *lower, columns)


def panels(z):
    chunks, rows, items = z.shape
    half = chunks // 2
    x, y = lax.axis_index(X), lax.axis_index("y")

    beside = around(z[:half], X)
    turned, beside = lax.optimization_barrier((swap(z, ROW), beside))
    own = swap(turned, PLANE)
    places = [((y + up) % 4, (x + on) % 4) for up in (0, 3, 1, 2) for on in (0, 3, 1, 2)]
    own = pick(own, [((at // 2) * 4 + up) * 2 + at % 2 for up, at in places]).reshape(16 * rows, items)
    own, beside, z = lax.optimization_barrier((own, beside, z))
    columns = lax.all_gather(own, ROW, tiled=True)

    line = jnp.stack((z[:half],) + beside, axis=1)
    tall = jnp.stack((z[half:],) + around(z[half:], "y"), axis=1)
    near_a = neighbours(line, "y")
    near_b = neighbours(tall, X)
    upper = (line,) + near_a + across(*near_a, "y")
    lower = (tall,) + near_b + across(*near_b, X)
    return gram(upper, lower, columns)


def pick(z, order):
    count, rows, items = z.shape
    source = (jnp.stack(order)[:, None] * rows + jnp.arange(rows)).reshape(-1, 1)
    chosen = (source == jnp.arange(count * rows)).astype(z.dtype)
    taken = jnp.dot(chosen, z.reshape(count * rows, items), preferred_element_type=jnp.float32)
    return taken.astype(z.dtype).reshape(z.shape)


def total(x, axis):
    return jnp.sum(swap(jnp.broadcast_to(x, (16,) + x.shape), axis), axis=0)


def swap(x, axis):
    return lax.all_to_all(x, axis, 0, 0, tiled=True)


def shards(responses, observed, qmatrix, guess, slip):
    learners, items = responses.shape
    cols, rows = 8, 16
    part = learners // cols
    chunk = part // rows

    right = (responses * observed).astype(jnp.bfloat16).reshape(cols, part, items)
    seen = observed.astype(jnp.bfloat16).reshape(cols, part, items)
    table = jnp.concatenate(
        [qmatrix.astype(jnp.float32).T, jnp.stack(triple(guess) + triple(slip)), jnp.zeros((2, items))]
    ).astype(jnp.bfloat16)
    table = jnp.broadcast_to(table, (cols,) + table.shape)
    mixed = swap(jnp.concatenate([right, seen, table], axis=1), COL)
    mixed = mixed.transpose(1, 0, 2).reshape(2 * part + 16, cols * items)
    right, seen, table = mixed[:part], mixed[part : 2 * part], mixed[2 * part :].astype(jnp.float32)
    needs = table[:ATTRS]
    guess = table[8] + table[9] + table[10]
    slip = table[11] + table[12] + table[13]

    codes = jnp.arange(PROFILES, dtype=jnp.int32)
    powers = jnp.arange(ATTRS, dtype=jnp.int32)
    bits = (codes[:, None] >> powers[None, :] & 1).astype(jnp.float32)
    lacking = jnp.dot(1.0 - bits, needs, precision=lax.Precision.HIGHEST)
    prob = jnp.where(lacking == 0.0, 1.0 - slip, guess)
    log0 = jnp.log(1.0 - prob)
    weights = jnp.concatenate([jnp.log(prob) - log0, log0], axis=1)
    data = jnp.concatenate([right, seen], axis=1)
    loglik = sum(
        lax.dot_general(data, w.astype(jnp.bfloat16), (((1,), (1,)), ((), ())), preferred_element_type=jnp.float32)
        for w in triple(weights)
    )
    loglik = loglik.reshape(rows // 2, 2, chunk, PROFILES)
    core = lax.axis_index("k")
    mine = lax.dynamic_index_in_dim(loglik, core, 1, keepdims=False)
    theirs = lax.dynamic_index_in_dim(loglik, 1 - core, 1, keepdims=False)
    loglik = jnp.sum(swap(mine + other_core(theirs), "z"), axis=0)
    posterior = jax.nn.softmax(loglik, axis=1).astype(jnp.bfloat16)
    posterior = swap(jnp.broadcast_to(posterior, (rows, chunk, PROFILES)), ROW).reshape(part, PROFILES)

    expected = jnp.dot(posterior, prob.astype(jnp.bfloat16), preferred_element_type=jnp.float32)
    seen = seen.astype(jnp.float32)
    resid = right.astype(jnp.float32) - seen * expected
    sums = total(jnp.stack([jnp.sum(seen, axis=0), jnp.sum(resid, axis=0), jnp.sum(resid * resid, axis=0)]), PLANE)
    count = jnp.maximum(sums[0], 1.0)
    mean = sums[1] / count
    var = sums[2] / count - mean * mean
    root = jnp.sqrt(jnp.sqrt(jnp.float32(learners * 2)))
    zres = (seen * (resid - mean) * (lax.rsqrt(var + 1e-06) * lax.rsqrt(count) * root)).astype(jnp.bfloat16)
    return panels(zres.reshape(rows, chunk, cols * items))


def solution(mesh):
    named = Mesh(mesh.devices.reshape(8, 2, 2, 4, 2), ("z", "k", "xh", "y", "xl"))
    items = ROW + COL
    placed = (P("xl", items), P("xl", items), P(items, None), P(items), P(items))
    return jax.shard_map(shards, mesh=named, in_specs=placed, out_specs=P(ROW, PLANE), check_vma=False)
```

```python
import jax
import jax.numpy as jnp
from jax import lax
from jax.experimental import pallas as pl
from jax.experimental.pallas import tpu as pltpu
from jax.sharding import Mesh, PartitionSpec as P

ATTRS = 8
PROFILES = 256

ROW = ("z", "k")
COL = ("xh", "y")
PLANE = ("xh", "y", "xl")
X = ("xh", "xl")


def shift(x, axis, n, by):
    return lax.ppermute(x, axis, [(i, (i + by) % n) for i in range(n)])


def triple(x):
    high = lax.reduce_precision(x, 8, 7)
    rest = x - high
    middle = lax.reduce_precision(rest, 8, 7)
    return high, middle, rest - middle


def around(x, axis):
    return shift(x, axis, 4, 1), shift(x, axis, 4, -1), shift(x, axis, 4, 2)


def other_core(x):
    return lax.ppermute(x, "k", [(0, 1), (1, 0)])


def neighbours(x, axis):
    return shift(x, axis, 4, 1), shift(x, axis, 4, -1)


def across(before, after, axis):
    half = before.shape[0] // 2
    return shift(before[:half], axis, 4, 1), shift(after[half:], axis, 4, -1)


def gram_kernel(upper, lower, columns, out, left):
    step = pl.program_id(0)
    for at in range(4):
        three, far = ((upper[:3], upper[3 + at]) if at < 2 else (lower[:3], lower[3 + at - 2]))

        @pl.when(step == at)
        def _():
            for i, piece in enumerate(tuple(three) + (far,)):
                if at < 2:
                    left[:, i] = piece[...]
                else:
                    left[:, :, i] = piece[...]

    term = lax.dot_general(
        left[...].reshape(columns.shape), columns[...], (((0,), (0,)), ((), ())), preferred_element_type=jnp.float32
    )

    @pl.when(step == 0)
    def _():
        out[...] = term

    @pl.when(step > 0)
    def _():
        out[...] += term


def gram(upper, lower, columns):
    learners, items = columns.shape
    rows = upper[0].shape[2]
    steps = 4
    block = (learners // steps // (16 * rows), 4, rows, items)
    pair = [
        pl.BlockSpec(block, lambda j: (jnp.minimum(j, 1), 0, 0, 0)),
        pl.BlockSpec(block, lambda j: (jnp.maximum(j - 2, 0), 0, 0, 0)),
    ]
    far = pl.BlockSpec(block, lambda j: (0, 0, 0, 0))
    return pl.pallas_call(
        lambda *refs: gram_kernel(refs[:5], refs[5:10], *refs[10:]),
        grid=(steps,),
        in_specs=[pair[0]] * 3 + [far] * 2 + [pair[1]] * 3 + [far] * 2
        + [pl.BlockSpec((learners // steps, items), lambda j: (j, 0))],
        out_specs=pl.BlockSpec((items, items), lambda j: (0, 0)),
        out_shape=jax.ShapeDtypeStruct((items, items), jnp.float32),
        scratch_shapes=[pltpu.VMEM((block[0], 4, 4, rows, items), jnp.bfloat16)],
        compiler_params=pltpu.CompilerParams(
            dimension_semantics=("arbitrary",), vmem_limit_bytes=56 * 2**20
        ),
        name="gram",
    )(*upper, *lower, columns)


def panels(z):
    chunks, rows, items = z.shape
    half = chunks // 2
    x, y = lax.axis_index(X), lax.axis_index("y")

    beside = around(z[:half], X)
    turned, beside = lax.optimization_barrier((swap(z, ROW), beside))
    own = swap(turned, PLANE)
    places = [((y + up) % 4, (x + on) % 4) for up in (0, 3, 1, 2) for on in (0, 3, 1, 2)]
    own = pick(own, [((at // 2) * 4 + up) * 2 + at % 2 for up, at in places]).reshape(16 * rows, items)
    own, beside, z = lax.optimization_barrier((own, beside, z))
    columns = lax.all_gather(own, ROW, tiled=True)

    line = jnp.stack((z[:half],) + beside, axis=1)
    tall = jnp.stack((z[half:],) + around(z[half:], "y"), axis=1)
    near_a = neighbours(line, "y")
    near_b = neighbours(tall, X)
    upper = (line,) + near_a + across(*near_a, "y")
    lower = (tall,) + near_b + across(*near_b, X)
    return gram(upper, lower, columns)


def pick(z, order):
    count, rows, items = z.shape
    source = (jnp.stack(order)[:, None] * rows + jnp.arange(rows)).reshape(-1, 1)
    chosen = (source == jnp.arange(count * rows)).astype(z.dtype)
    taken = jnp.dot(chosen, z.reshape(count * rows, items), preferred_element_type=jnp.float32)
    return taken.astype(z.dtype).reshape(z.shape)


def total(x, axis):
    return jnp.sum(swap(jnp.broadcast_to(x, (16,) + x.shape), axis), axis=0)


def swap(x, axis):
    return lax.all_to_all(x, axis, 0, 0, tiled=True)


def pack_kernel(responses, observed, needs, guess, slip, out):
    parts, part, items = responses.shape
    for at in range(parts):
        seen = observed[at]
        out[at, :part] = (responses[at] * seen).astype(jnp.float32).astype(jnp.bfloat16)
        out[at, part : 2 * part] = seen.astype(jnp.float32).astype(jnp.bfloat16)
    row = lax.broadcasted_iota(jnp.int32, (8, items), 0)
    terms = jnp.zeros((8, items), jnp.float32)
    for first, value in ((0, guess[...]), (3, slip[...])):
        for at in range(3):
            term = value.astype(jnp.bfloat16).astype(jnp.float32)
            terms = jnp.where(row == first + at, term, terms)
            value = value - term
    table = jnp.concatenate([needs[...].astype(jnp.float32), terms], axis=0)
    for at in range(parts):
        out[at, 2 * part :] = table.astype(jnp.bfloat16)


def packed(responses, observed, qmatrix, guess, slip, cols):
    learners, items = responses.shape
    part = learners // cols
    steps = 2
    data = pl.BlockSpec((cols // steps, part, items), lambda j: (j, 0, 0))
    needs = pl.BlockSpec((ATTRS, items), lambda j: (0, 0))
    line = pl.BlockSpec((1, items), lambda j: (0, 0))
    rows = 2 * part + 16
    return pl.pallas_call(
        pack_kernel,
        grid=(steps,),
        in_specs=[data, data, needs, line, line],
        out_specs=pl.BlockSpec((cols // steps, rows, items), lambda j: (j, 0, 0)),
        out_shape=jax.ShapeDtypeStruct((cols, rows, items), jnp.bfloat16),
        compiler_params=pltpu.CompilerParams(dimension_semantics=("arbitrary",)),
        name="pack",
    )(responses.reshape(cols, part, items), observed.reshape(cols, part, items), qmatrix.T, guess[None], slip[None])


def shards(responses, observed, qmatrix, guess, slip):
    learners, items = responses.shape
    cols, rows = 8, 16
    part = learners // cols
    chunk = part // rows

    mixed = swap(packed(responses, observed, qmatrix, guess, slip, cols), COL)
    mixed = mixed.transpose(1, 0, 2).reshape(2 * part + 16, cols * items)
    right, seen, table = mixed[:part], mixed[part : 2 * part], mixed[2 * part :].astype(jnp.float32)
    needs = table[:ATTRS]
    guess = table[8] + table[9] + table[10]
    slip = table[11] + table[12] + table[13]

    codes = jnp.arange(PROFILES, dtype=jnp.int32)
    powers = jnp.arange(ATTRS, dtype=jnp.int32)
    bits = (codes[:, None] >> powers[None, :] & 1).astype(jnp.float32)
    lacking = jnp.dot(1.0 - bits, needs, precision=lax.Precision.HIGHEST)
    prob = jnp.where(lacking == 0.0, 1.0 - slip, guess)
    log0 = jnp.log(1.0 - prob)
    weights = jnp.concatenate([jnp.log(prob) - log0, log0], axis=1)
    data = jnp.concatenate([right, seen], axis=1)
    loglik = sum(
        lax.dot_general(data, w.astype(jnp.bfloat16), (((1,), (1,)), ((), ())), preferred_element_type=jnp.float32)
        for w in triple(weights)
    )
    loglik = loglik.reshape(rows // 2, 2, chunk, PROFILES)
    core = lax.axis_index("k")
    mine = lax.dynamic_index_in_dim(loglik, core, 1, keepdims=False)
    theirs = lax.dynamic_index_in_dim(loglik, 1 - core, 1, keepdims=False)
    loglik = jnp.sum(swap(mine + other_core(theirs), "z"), axis=0)
    posterior = jax.nn.softmax(loglik, axis=1).astype(jnp.bfloat16)
    posterior = swap(jnp.broadcast_to(posterior, (rows, chunk, PROFILES)), ROW).reshape(part, PROFILES)

    expected = jnp.dot(posterior, prob.astype(jnp.bfloat16), preferred_element_type=jnp.float32)
    seen = seen.astype(jnp.float32)
    resid = right.astype(jnp.float32) - seen * expected
    sums = total(jnp.stack([jnp.sum(seen, axis=0), jnp.sum(resid, axis=0), jnp.sum(resid * resid, axis=0)]), PLANE)
    count = jnp.maximum(sums[0], 1.0)
    mean = sums[1] / count
    var = sums[2] / count - mean * mean
    root = jnp.sqrt(jnp.sqrt(jnp.float32(learners * 2)))
    zres = (seen * (resid - mean) * (lax.rsqrt(var + 1e-06) * lax.rsqrt(count) * root)).astype(jnp.bfloat16)
    return panels(zres.reshape(rows, chunk, cols * items))


def solution(mesh):
    named = Mesh(mesh.devices.reshape(8, 2, 2, 4, 2), ("z", "k", "xh", "y", "xl"))
    items = ROW + COL
    placed = (P("xl", items), P("xl", items), P(items, None), P(items), P(items))
    return jax.shard_map(shards, mesh=named, in_specs=placed, out_specs=P(ROW, PLANE), check_vma=False)
```
